256 devices in a mesh: gx: 8 (over x, core), gy: 32 (over y, z).
Axes of the slice: x: 4, y: 4, z: 8, core: 2. Of those that a mesh axis runs over, the one named last changes fastest.
Arguments:
- reference_image: bfloat16 [32, 256, 4096], P(None, 'gx', 'gy'), may hold values from -6 to 6
- moving_image: float32 [44, 256, 4096], P(None, 'gx', 'gy'), may hold values from -6 to 6
- image_gradient: bfloat16 [3, 32, 256, 4096], P(None, None, 'gx', 'gy'), may hold values from -1.5 to 1.5
- voxel_shift: int32 [3, 4, 32, 512], P(None, None, 'gx', 'gy'), may hold values from -6 to 5
- subvoxel: float32 [3, 4, 32, 512], P(None, None, 'gx', 'gy'), may hold values from 0 to 1
Outputs:
- increment: float32 [3, 5, 32, 512], P(None, None, 'gx', 'gy')
- cg_residual: float32 [3, 5, 32, 512], P(None, None, 'gx', 'gy')
The draws below stay inside these ranges and needn't reach their ends.
All inputs are finite; a program needn't handle non-finite values.
Results may differ from the reference program's by a relative error of at most 0.0003.
Values sent between devices are 32-bit elements; how exact they have to be, the bound alone decides.
No kernel may reach another device: no remote copies, remote signals or barrier semaphores. Data moves between devices by JAX's collectives and lax.ppermute only.
A program may use at most 128 MiB of HBM per device.

```python
import jax
import jax.numpy as jnp
from jax import lax

CZ = 32
ELEM = 8
HW = 6
ITERS = 3
NX = 256
NY = 4096
GZ = 44
NZE = 4
NXE = 32
NYE = 512


def plant(array, key, least, high):
    place = [jax.random.randint(jax.random.fold_in(key, axis), (), 0, length) for axis, length in enumerate(array.shape)]
    widest = array.shape.index(max(array.shape))
    next_to = place[:widest] + [(place[widest] + 1) % array.shape[widest]] + place[widest + 1:]
    return array.at[tuple(place)].set(least).at[tuple(next_to)].set(high)


def steps_of(stream_key, shape, split, least, top_value):
    def one(position, shards_of):
        draws = jax.random.uniform(jax.random.fold_in(jax.random.fold_in(stream_key, 6), position), (shards_of,), jnp.float32, least / len(split), top_value / len(split))
        return jnp.repeat(jnp.exp(draws), shape[position] // shards_of).reshape((-1,) + (1,) * (len(shape) - position - 1))

    gain = one(*split[0])
    for cut in split[1:]:
        gain = gain * one(*cut)
    return gain


def centred(own_key, extent, width, limit, cuts=(), kind=jnp.bfloat16):
    values = width * jax.random.normal(own_key, extent, jnp.float32)
    if cuts:
        values = values * steps_of(own_key, extent, cuts, -0.22, 0.18)
    return jnp.clip(values, -limit, limit).astype(kind)


def setup_inputs(seed: int = 0) -> dict:
    key_list = jax.random.split(jax.random.key(seed), 6)
    reference_image = centred(key_list[0], (CZ, NX, NY), 1.0, 6.0, ((1, 8), (2, 32)))
    moving_image = centred(key_list[1], (GZ, NX, NY), 1.0, 6.0, ((1, 8), (2, 32)), jnp.float32)
    image_gradient = centred(key_list[2], (3, CZ, NX, NY), 0.25, 1.5, ((2, 8), (3, 32)))
    voxel_shift = plant(jax.random.randint(key_list[3], (3, NZE, NXE, NYE), -HW, HW), jax.random.fold_in(key_list[3], 1), -HW, HW - 1).astype(jnp.int32)
    subvoxel = jnp.clip(1.0 * jax.random.uniform(key_list[4], (3, NZE, NXE, NYE), jnp.float32) ** steps_of(key_list[4], (3, NZE, NXE, NYE), ((2, 8), (3, 32)), -0.2, 0.2), 0.0, 1.0)
    return dict(reference_image=reference_image, moving_image=moving_image, image_gradient=image_gradient, voxel_shift=voxel_shift, subvoxel=subvoxel)


ridge_weight = 2.0


def linear_basis():
    centres = (jnp.arange(ELEM, dtype=jnp.float32) + 0.5) / ELEM
    return jnp.stack([1.0 - centres, centres])


def corner_sides():
    return [(side_z, side_x, side_y) for side_z in (0, 1) for side_x in (0, 1) for side_y in (0, 1)]


def element_view(volume):
    extent_z, extent_x, extent_y = volume.shape
    return volume.reshape(extent_z // ELEM, ELEM, extent_x // ELEM, ELEM, extent_y // ELEM, ELEM)


def element_stiffness(gradient):
    shape_basis = linear_basis()
    basis_pairs = shape_basis[:, None, :] * shape_basis[None, :, :]
    blocks = {}
    for first_comp in range(3):
        for second_comp in range(first_comp, 3):
            product = gradient[first_comp].astype(jnp.float32) * gradient[second_comp].astype(jnp.float32)
            summed = jnp.einsum("zixjyl,pqi,rsj,tul->prtqsuzxy", element_view(product), basis_pairs, basis_pairs, basis_pairs, precision=lax.Precision.HIGHEST)
            blocks[(first_comp, second_comp)] = summed.reshape(8, 8, -1)
            blocks[(second_comp, first_comp)] = blocks[(first_comp, second_comp)]
    stiff_rows = []
    for first_comp in range(3):
        stiff_rows.append(jnp.stack([blocks[(first_comp, second_comp)] for second_comp in range(3)], axis=2))
    return jnp.stack(stiff_rows, axis=1)


def element_load(image, gradient, warped):
    shape_basis = linear_basis()
    mismatch = image.astype(jnp.float32) - warped
    load_terms = []
    for component in range(3):
        weighted = gradient[component].astype(jnp.float32) * mismatch
        summed = jnp.einsum("zixjyl,pi,qj,rl->pqrzxy", element_view(weighted), shape_basis, shape_basis, shape_basis, precision=lax.Precision.HIGHEST)
        load_terms.append(summed.reshape(8, -1))
    return jnp.stack(load_terms, axis=1)


def warp_blocks(padded, voxel_shift, subvoxel, x_anchor, y_anchor):
    count_z = voxel_shift.shape[1]
    count_x = voxel_shift.shape[2]
    count_y = voxel_shift.shape[3]
    index_z = jnp.arange(count_z, dtype=jnp.int32)[:, None, None] * ELEM
    index_x = jnp.arange(count_x, dtype=jnp.int32)[None, :, None] * ELEM + x_anchor
    index_y = jnp.arange(count_y, dtype=jnp.int32)[None, None, :] * ELEM + y_anchor
    start_z = (index_z + voxel_shift[0] + HW).astype(jnp.int32).reshape(-1)
    start_x = (index_x + voxel_shift[1] + HW).astype(jnp.int32).reshape(-1)
    start_y = (index_y + voxel_shift[2] + HW).astype(jnp.int32).reshape(-1)

    def cut_block(corner_z, corner_x, corner_y):
        return lax.dynamic_slice(padded, (corner_z, corner_x, corner_y), (ELEM + 1, ELEM + 1, ELEM + 1))

    gathered = jax.vmap(cut_block, out_axes=3)(start_z, start_x, start_y)
    weight_z = subvoxel[0].reshape(-1)
    weight_x = subvoxel[1].reshape(-1)
    weight_y = subvoxel[2].reshape(-1)
    along_z = (1.0 - weight_z) * gathered[:ELEM] + weight_z * gathered[1:]
    along_x = (1.0 - weight_x) * along_z[:, :ELEM] + weight_x * along_z[:, 1:]
    along_y = (1.0 - weight_y) * along_x[:, :, :ELEM] + weight_y * along_x[:, :, 1:]
    shaped = along_y.reshape(ELEM, ELEM, ELEM, count_z, count_x, count_y)
    return shaped.transpose(3, 0, 4, 1, 5, 2).reshape(count_z * ELEM, count_x * ELEM, count_y * ELEM)


def nodes_to_elements(nodal_field, count_z, count_x, count_y):
    picked = [nodal_field[:, side_z:side_z + count_z, side_x:side_x + count_x, side_y:side_y + count_y] for (side_z, side_x, side_y) in corner_sides()]
    return jnp.stack(picked).reshape(8, 3, -1)


def elements_to_nodes(element_terms, count_z, count_x, count_y):
    shaped = element_terms.reshape(8, 3, count_z, count_x, count_y)
    nodal_sum = jnp.zeros((3, count_z + 1, count_x + 1, count_y + 1), jnp.float32)
    for corner_index, (side_z, side_x, side_y) in enumerate(corner_sides()):
        nodal_sum = nodal_sum + jnp.pad(shaped[corner_index], ((0, 0), (side_z, 1 - side_z), (side_x, 1 - side_x), (side_y, 1 - side_y)))
    return nodal_sum


def element_product(stiffness, element_values):
    return jnp.sum(stiffness * element_values[None, None], axis=(2, 3))


def reference(reference_image, moving_image, image_gradient, voxel_shift, subvoxel):
    count_z = CZ // ELEM
    count_x = NX // ELEM
    count_y = NY // ELEM
    padded = jnp.pad(moving_image, ((0, 0), (HW, HW), (HW, HW)))
    image_rows = reference_image.reshape(CZ, count_x, ELEM, NY).transpose(1, 0, 2, 3)
    gradient_rows = image_gradient.reshape(3, CZ, count_x, ELEM, NY).transpose(2, 0, 1, 3, 4)
    shift_rows = voxel_shift.transpose(2, 0, 1, 3)[:, :, :, None, :]
    frac_rows = subvoxel.transpose(2, 0, 1, 3)[:, :, :, None, :]
    anchors = jnp.arange(count_x, dtype=jnp.int32) * ELEM

    def one_row(inputs):
        image_row, gradient_row, shift_row, frac_row, anchor = inputs
        warped = warp_blocks(padded, shift_row, frac_row, anchor, 0)
        return element_stiffness(gradient_row), element_load(image_row, gradient_row, warped)

    stiff_map, load_map = lax.map(one_row, (image_rows, gradient_rows, shift_rows, frac_rows, anchors))
    stiffness = jnp.moveaxis(stiff_map.reshape(count_x, 8, 3, 8, 3, count_z, count_y), 0, 5).reshape(8, 3, 8, 3, -1)
    load_flat = jnp.moveaxis(load_map.reshape(count_x, 8, 3, count_z, count_y), 0, 3).reshape(8, 3, -1)
    load_nodes = elements_to_nodes(load_flat, count_z, count_x, count_y)

    def apply_operator(nodal_field):
        element_values = nodes_to_elements(nodal_field, count_z, count_x, count_y)
        return elements_to_nodes(element_product(stiffness, element_values), count_z, count_x, count_y) + ridge_weight * nodal_field

    solution = jnp.zeros_like(load_nodes)
    residual = load_nodes
    direction = load_nodes
    norm_now = jnp.sum(residual * residual)
    for iteration in range(ITERS):
        image_dir = apply_operator(direction)
        step_length = norm_now / jnp.sum(direction * image_dir)
        solution = solution + step_length * direction
        residual = residual - step_length * image_dir
        norm_next = jnp.sum(residual * residual)
        direction = residual + (norm_next / norm_now) * direction
        norm_now = norm_next
    return solution[:, :, :count_x, :count_y], residual[:, :, :count_x, :count_y]
```

```python
import functools

import jax
import jax.numpy as jnp
import numpy as np
from jax import lax
from jax.experimental import pallas as pl
from jax.experimental.pallas import tpu as pltpu
from jax.sharding import Mesh
from jax.sharding import PartitionSpec as P

ELEM = 8
HW = 6
RIDGE = 2.0
GX = ("gx_0", "gx_1")
GY = ("gy_0", "gy_1")

CZ, CX, CY = 4, 4, 16
ZS = 24
LOW, HIGH = 3, 2
PAIRS = ((0, 0), (0, 1), (0, 2), (1, 1), (1, 2), (2, 2))
ROWS = 96
BF = jnp.bfloat16
F32 = jnp.float32

T = (np.arange(ELEM) + 0.5) / ELEM
PHI = np.stack([1.0 - T, T])
QUAD = np.stack([PHI[0] * PHI[0], PHI[0] * PHI[1], PHI[1] * PHI[1]])


def quad_of(p, q):
    return p + q


def bf(a):
    return jnp.asarray(np.asarray(a, np.float32), BF)


def stiff_y_weights():
    w = np.zeros((CZ * 128, 3 * 128))
    for ez in range(CZ):
        for r in range(3):
            for ey in range(CY):
                w[ez * 128 + ey * 8 : ez * 128 + ey * 8 + 8, r * 128 + ez * ZS + ey + LOW] = QUAD[r]
    return w


def stiff_x_weights():
    w = np.zeros((160, 96))
    for zq in range(3):
        for q in range(3):
            for ex in range(CX):
                cols = slice(zq * 32 + ex * 8, zq * 32 + ex * 8 + 8)
                w[(zq * 3 + q) * 8 + LOW + ex, cols] = QUAD[q]
                if ex >= 1:
                    w[96 + (ex - 1) * 9 + zq * 3 + q, cols] = QUAD[q]
                if ex < 2:
                    w[128 + ex * 9 + zq * 3 + q, cols] = QUAD[q]
    return w


def place_x():
    lo = np.zeros((ROWS, 32))
    hi = np.zeros((ROWS, 32))
    for f in range(9):
        for m in range(3):
            lo[f * 8 + m, m * 9 + f] = 1.0
        hi[f * 8 + 7, f] = 1.0
        hi[72 + f, 9 + f] = 1.0
    return lo, hi


def pack_y():
    w = np.zeros((3 * 384, 256))
    for j in range(3):
        for r in range(3):
            for z in range(CZ):
                for m in range(3):
                    w[j * 384 + r * 128 + z * ZS + LOW + 13 + m, j * 36 + r * 12 + z * 3 + m] = 1.0
                for m in range(2):
                    w[j * 384 + r * 128 + z * ZS + LOW + m, 128 + j * 36 + r * 12 + z * 3 + m] = 1.0
    return w


def place_y():
    w = np.zeros((3, 256, 384))
    for j in range(3):
        for r in range(3):
            for z in range(CZ):
                for m in range(3):
                    w[j, j * 36 + r * 12 + z * 3 + m, r * 128 + z * ZS + m] = 1.0
                for m in range(2):
                    w[j, 128 + j * 36 + r * 12 + z * 3 + m, r * 128 + z * ZS + LOW + CY + m] = 1.0
    return w


def load_y_weights():
    w = np.zeros((2 * CZ * 128, 128))
    for side in range(2):
        for ez in range(CZ):
            base = (side * CZ + ez) * 128
            for ey in range(CY):
                for c in range(2):
                    w[base + ey * 8 : base + ey * 8 + 8, (ez + side) * ZS + LOW + ey + c] += PHI[c]
    return w


def load_x_weights():
    w = np.zeros((8, 32))
    for ex in range(CX):
        for b in range(2):
            w[LOW + ex + b, ex * 8 : ex * 8 + 8] += PHI[b]
    return w


def split3(x):
    h = x.astype(BF)
    r = x - h.astype(F32)
    m = r.astype(BF)
    return h, m, (r - m.astype(F32)).astype(BF)


def dot(a, b):
    return jnp.dot(a, b, preferred_element_type=F32)


def dot_right(x, w):
    h, m, l = split3(x)
    return (dot(l, w) + dot(m, w)) + dot(h, w)


def dot_left(w, x):
    h, m, l = split3(x)
    return (dot(w, l) + dot(w, m)) + dot(w, h)


def stiff_kernel(grad, wy, wx, own, up, low, q_acc):
    def step(ez, carry):
        for xb in range(2):
            acc = [[None] * 3 for _ in PAIRS]
            for i in range(ELEM):
                g = [grad[k, ez * ELEM + i, xb * 16 : xb * 16 + 16, :].astype(F32) for k in range(3)]
                for n, (a, b) in enumerate(PAIRS):
                    prod = g[a] * g[b]
                    for zq in range(3):
                        term = prod * float(QUAD[zq, i])
                        acc[n][zq] = term if i == 0 else acc[n][zq] + term
            for n in range(6):
                for zq in range(3):
                    row = (n * 3 + zq) * 32 + xb * 16
                    q_acc[row : row + 16, pl.ds(pl.multiple_of(ez * 128, 128), 128)] = acc[n][zq]
        return carry

    lax.fori_loop(0, CZ, step, 0)
    for n in range(6):
        d = dot_right(q_acc[n * 96 : n * 96 + 96, :], wy[...])
        o = dot_left(wx[...], d)
        own[n] = o[:96]
        up[n] = o[96:128]
        low[n] = o[128:160]


def extend_kernel(own, from_low, from_up, plo, phi, pack, ext, y_up, y_low):
    for g in range(2):
        packed = None
        for j in range(3):
            n = g * 3 + j
            s = own[n] + dot_left(plo[...], from_low[n]) + dot_left(phi[...], from_up[n])
            ext[n] = s
            part = dot_right(s, pack[j * 384 : j * 384 + 384, :])
            packed = part if packed is None else packed + part
        y_up[g] = packed[:, :128]
        y_low[g] = packed[:, 128:]


def strip_kernel(mov, from_low, from_up, y_up, y_low):
    lane = lax.broadcasted_iota(jnp.int32, (48, 128), 1)
    group = lane >> 3
    for zz in range(3):
        acc_up = jnp.zeros((48, 128), F32)
        acc_low = jnp.zeros((48, 128), F32)
        for g in range(16):
            z = zz * 16 + g
            if z >= mov.shape[0]:
                break
            rows = jnp.concatenate([from_low[z], mov[z], from_up[z]], axis=0)
            sel = group == g
            acc_up = jnp.where(sel, pltpu.roll(rows, (8 * g + 8) % 128, 1) if (8 * g + 8) % 128 else rows, acc_up)
            acc_low = jnp.where(sel, pltpu.roll(rows, 8 * g, 1) if g else rows, acc_low)
        y_up[zz] = acc_up
        y_low[zz] = acc_low


def warp_kernel(shift, frac, mov, x_low, x_up, y_low, y_up, image, grad, wly, wlx, load, vol, zz_acc):
    lane = lax.broadcasted_iota(jnp.int32, (8, 128), 1)
    group = lane >> 3
    lane48 = lax.broadcasted_iota(jnp.int32, (48, 128), 1)

    for z in range(mov.shape[0]):
        rows = jnp.concatenate([x_low[z], mov[z], x_up[z]], axis=0)
        vol[0, z] = rows
        zb, g = z // 16, z % 16
        sl, su = y_low[zb], y_up[zb]
        left = pltpu.roll(sl, 128 - 8 * g, 1) if g else sl
        right = pltpu.roll(su, 120 - 8 * g, 1) if g != 15 else su
        edge = jnp.where(lane48 < 64, pltpu.roll(rows, 8, 1), pltpu.roll(rows, 120, 1))
        edge = jnp.where(lane48 < 8, left, edge)
        vol[1, z] = jnp.where(lane48 >= 120, right, edge)

    n_elem = CZ * CX * CY

    def step(it, carry):
        ez = it // 2
        xp = it % 2
        for h in range(2):
            lo = [None] * ELEM
            hi = [None] * ELEM
            wyv = None
            ex = xp * 2 + h
            for ey in range(CY):
                e = (ez * CX + ex) * CY + ey
                z0 = ez * ELEM + shift[e] + HW
                x0 = ex * ELEM + shift[n_elem + e] + 8
                sy = shift[2 * n_elem + e]
                wz, wx, wy = frac[e], frac[n_elem + e], frac[2 * n_elem + e]
                uz, ux = 1.0 - wz, 1.0 - wx
                if ey == 0:
                    tile, amount = 1, 120 - sy
                elif ey == CY - 1:
                    tile, amount = 1, 136 - sy
                else:
                    tile, amount = 0, 128 - sy
                amount_lo = amount & 127
                amount_hi = (amount - 1) & 127
                sel = group == ey
                wyv = jnp.full((8, 128), wy, F32) if ey == 0 else jnp.where(sel, wy, wyv)
                prev = None
                for i in range(ELEM + 1):
                    a = vol[tile, z0 + i, pl.ds(x0, 8), :]
                    b = vol[tile, z0 + i, pl.ds(x0 + 1, 8), :]
                    c = ux * a + wx * b
                    if i:
                        d = uz * prev + wz * c
                        r_lo = pltpu.roll(d, amount_lo, 1)
                        r_hi = pltpu.roll(d, amount_hi, 1)
                        j = i - 1
                        lo[j] = r_lo if ey == 0 else jnp.where(sel, r_lo, lo[j])
                        hi[j] = r_hi if ey == 0 else jnp.where(sel, r_hi, hi[j])
                    prev = c
            uyv = 1.0 - wyv
            x_rows = pl.ds(pl.multiple_of(xp * 16, 16), 16)
            sums = [[None, None] for _ in range(3)]
            for i in range(ELEM):
                warped = uyv * lo[i] + wyv * hi[i]
                z = ez * ELEM + i
                img = image[z, x_rows, :].astype(F32)[h * 8 : h * 8 + 8]
                miss = img - warped
                for k in range(3):
                    gk = grad[k, z, x_rows, :].astype(F32)[h * 8 : h * 8 + 8]
                    prod = gk * miss
                    for side in range(2):
                        term = prod * float(PHI[side, i])
                        sums[k][side] = term if i == 0 else sums[k][side] + term
            for k in range(3):
                for side in range(2):
                    rows8 = pl.ds(pl.multiple_of(k * 32 + xp * 16 + h * 8, 8), 8)
                    zz_acc[rows8, pl.ds(pl.multiple_of((side * CZ + ez) * 128, 128), 128)] = sums[k][side]
        return carry

    lax.fori_loop(0, CZ * 2, step, 0)
    t = dot_right(zz_acc[...], wly[...])
    for k in range(3):
        load[k] = dot_left(wlx[...], t[k * 32 : k * 32 + 32])


def two_sum(a, b):
    s = a + b
    t = s - a
    return s, (a - (s - t)) + (b - t)


def fast_two_sum(a, b):
    s = a + b
    return s, b - (s - a)


def halves(a):
    c = a * 4097.0
    h = c - (c - a)
    return h, a - h


def two_prod(a, b):
    p = a * b
    ah, al = halves(a)
    bh, bl = halves(b)
    return p, ((ah * bh - p) + ah * bl + al * bh) + al * bl


def df_add(x, y):
    s, e = two_sum(x[0], y[0])
    t, f = two_sum(x[1], y[1])
    s, e = fast_two_sum(s, e + t)
    return fast_two_sum(s, e + f)


def df_neg(x):
    return -x[0], -x[1]


def df_sub(x, y):
    return df_add(x, df_neg(y))


def df_mul(x, y):
    p, e = two_prod(x[0], y[0])
    return fast_two_sum(p, e + (x[0] * y[1] + x[1] * y[0]))


def df_div(x, y):
    q1 = x[0] / y[0]
    p = df_mul(y, (q1, jnp.zeros_like(q1)))
    r = df_sub(x, p)
    q2 = r[0] / y[0]
    return fast_two_sum(q1, q2)


def corner_index(a, b, c):
    return a * 4 + b * 2 + c


def gather_corners(low_rows, high_rows):
    out = {}
    for k in range(3):
        for b, base in enumerate((low_rows[k], high_rows[k])):
            for a in range(2):
                for c in range(2):
                    s = a * ZS + c
                    out[corner_index(a, b, c), k] = pltpu.roll(base, 128 - s, 1) if s else base
    return out


def product(coef, values):
    acc = {}
    for n, (k1, k2) in enumerate(PAIRS):
        for zq in range(3):
            for q in range(3):
                for r in range(3):
                    s = coef(n, zq, q, r)
                    for a in ((0, 0), (0, 1), (1, 0), (1, 1)):
                        if sum(a) != zq:
                            continue
                        for b in ((0, 0), (0, 1), (1, 0), (1, 1)):
                            if sum(b) != q:
                                continue
                            for c in ((0, 0), (0, 1), (1, 0), (1, 1)):
                                if sum(c) != r:
                                    continue
                                to = corner_index(a[0], b[0], c[0])
                                of = corner_index(a[1], b[1], c[1])
                                for i, j in ((k1, k2),) if k1 == k2 else ((k1, k2), (k2, k1)):
                                    term = s * values[of, j]
                                    key = (to, i)
                                    acc[key] = term if key not in acc else acc[key] + term
    return acc


def fold_lanes(acc, k, b):
    total = acc[corner_index(0, b, 0), k]
    for a, c in ((0, 1), (1, 0), (1, 1)):
        total = total + pltpu.roll(acc[corner_index(a, b, c), k], a * ZS + c, 1)
    return total


def krylov_kernel(last, v_own, v_low, v_up, ext, p_low, p_up, place, basis, sums, coefs):
    lane = lax.broadcasted_iota(jnp.int32, (16, 128), 1)
    layer = jnp.zeros((16, 128), jnp.int32)
    for z in range(1, 6):
        layer = layer + (lane >= z * ZS).astype(jnp.int32)
    y = lane - layer * ZS - LOW
    inside = layer < 5
    take_low = inside & (y >= -LOW) & (y <= 0)
    take_up = inside & (y >= CY) & (y <= CY + 2)

    for n in range(6):
        both = jnp.concatenate([p_low[n // 3], p_up[n // 3]], axis=1)
        coefs[n * ROWS : n * ROWS + ROWS, :] = ext[n] + dot_right(both, place[n % 3])

    def coef_main(n, zq, q, r):
        row = n * ROWS + (zq * 3 + q) * 8
        return coefs[row : row + 8, r * 128 : r * 128 + 128]

    def coef_last(n, zq, q, r):
        row = n * ROWS + 72 + zq * 3 + q
        return jnp.broadcast_to(coefs[row : row + 1, r * 128 : r * 128 + 128], (8, 128))

    v0 = []
    for k in range(3):
        t = v_own[k]
        t = t + jnp.where(take_low, pltpu.roll(v_low[k], 128 - CY, 1), 0.0)
        t = t + jnp.where(take_up, pltpu.roll(v_up[k], CY, 1), 0.0)
        v0.append(t)
    low_rows = [t[0:8] for t in v0]
    high_rows = [t[1:9] for t in v0]
    end_low = [jnp.broadcast_to(t[8:9], (8, 128)) for t in v0]
    end_high = [jnp.broadcast_to(t[9:10], (8, 128)) for t in v0]

    sub = lax.broadcasted_iota(jnp.int32, (8, 128), 0)
    y8 = y[0:8]
    owned = inside[0:8] & (sub >= LOW) & (sub < LOW + CX + last[0]) & (y8 >= 0) & (y8 < CY + last[1])

    vs = [low_rows]
    extra = product(coef_last, gather_corners(end_low, end_high))
    for it in range(3):
        acc = product(coef_main, gather_corners(low_rows, high_rows))
        new_low, new_high = [], []
        for k in range(3):
            o0 = fold_lanes(acc, k, 0)
            o1 = fold_lanes(acc, k, 1)
            new_low.append(o0 + pltpu.roll(o1, 1, 0))
            if it < 2:
                shifted = pltpu.roll(o0, 7, 0)
                if it == 0:
                    shifted = jnp.where(sub == 7, fold_lanes(extra, k, 0), shifted)
                new_high.append(shifted + o1)
        low_rows, high_rows = new_low, new_high
        vs.append(low_rows)

    for i in range(4):
        for k in range(3):
            basis[i, k] = vs[i][k]

    zero = jnp.zeros((8, 128), F32)
    high = zero
    low = zero
    for j in range(6):
        a, b = vs[j // 2], vs[(j + 1) // 2]
        total = None
        for k in range(3):
            p, e = two_prod(jnp.where(owned, a[k], 0.0), b[k])
            term = (jnp.where(owned, p, 0.0), jnp.where(owned, e, 0.0))
            total = term if total is None else df_add(total, term)
        for s in (4, 2, 1):
            total = df_add(total, (pltpu.roll(total[0], s, 0), pltpu.roll(total[1], s, 0)))
        high = jnp.where(sub == j, total[0], high)
        low = jnp.where(sub == j, total[1], low)
    total = (high, low)
    for s in (64, 32, 16, 8, 4, 2, 1):
        total = df_add(total, (pltpu.roll(total[0], s, 1), pltpu.roll(total[1], s, 1)))
    lane8 = lane[0:8]
    row = jnp.where(lane8 == sub, total[0], 0.0) + jnp.where(lane8 == sub + 8, total[1], 0.0)
    row = jnp.sum(row, axis=0, keepdims=True)
    sums[...] = jnp.broadcast_to(row, sums.shape)


def add_rows(rows):
    lane = lax.broadcasted_iota(jnp.int32, rows.shape, 1)
    lows = pltpu.roll(rows, 120, 1)
    total = (jnp.where(lane < 8, rows, 0.0), jnp.where(lane < 8, lows, 0.0))
    n = rows.shape[0]
    while n > 8:
        n //= 2
        total = df_add((total[0][:n], total[1][:n]), (total[0][n:], total[1][n:]))
    s = n // 2
    while s >= 1:
        total = df_add(total, (pltpu.roll(total[0], s, 0), pltpu.roll(total[1], s, 0)))
        s //= 2
    return total


def partial_kernel(rows, out):
    high, low = add_rows(rows[...])
    row = high + pltpu.roll(low, 8, 1)
    out[...] = jnp.broadcast_to(row[0:1], out.shape)


def finish_kernel(rows, basis, inc, res):
    high, low = add_rows(rows[...])
    high, low = high[0:1], low[0:1]
    lane = lax.broadcasted_iota(jnp.int32, (1, 128), 1)

    def splat(part, j):
        return jnp.sum(jnp.where(lane == j, part, 0.0), axis=1, keepdims=True) + jnp.zeros((8, 128), F32)

    m = [(splat(high, j), splat(low, j)) for j in range(6)]
    m = [None] + [df_div(x, m[0]) for x in m[1:]]
    mu = m[1]
    lag = {j: df_sub(m[j], df_mul(mu, m[j - 1])) for j in range(2, 6)}
    n2 = lag[2]
    lag = {j: df_sub(lag[j], df_mul(mu, lag[j - 1])) for j in range(3, 6)}
    n3 = df_sub(lag[3], df_mul(mu, n2))
    lag = {j: df_sub(lag[j], df_mul(mu, lag[j - 1])) for j in range(4, 6)}
    n4 = df_sub(lag[4], df_mul(mu, n3))
    n5 = df_sub(df_sub(lag[5], df_mul(mu, lag[4])), df_mul(mu, n4))
    a1 = df_div(n3, n2)
    h2 = df_sub(df_sub(n4, df_mul(a1, n3)), df_mul(n2, n2))
    b2 = df_div(h2, n2)
    t = df_sub(df_sub(n5, df_mul(a1, n4)), df_mul(n2, n3))
    a2 = df_sub(df_div(t, h2), a1)
    two = (jnp.full((8, 128), RIDGE, F32), jnp.zeros((8, 128), F32))
    y0 = df_neg(df_add(two, mu))
    p2 = df_sub(df_mul(df_sub(y0, a1), y0), n2)
    p3 = df_sub(df_mul(df_sub(y0, a2), p2), df_mul(b2, y0))
    c2 = df_neg(df_add(a1, a2))
    c1 = df_sub(df_sub(df_mul(a1, a2), n2), b2)
    c0 = df_mul(a2, n2)
    q1 = df_add(y0, c2)
    q0 = df_add(df_mul(y0, q1), c1)
    s = 1.0 / p3[0]
    r3, r2, r1, r0 = s, s * c2[0], s * c1[0], s * c0[0]
    u2, u1, u0 = -s, -s * q1[0], -s * q0[0]
    mu = mu[0]
    for k in range(3):
        v = [basis[i, k] for i in range(4)]
        w1 = v[1] - mu * v[0]
        w2a = v[2] - mu * v[1]
        w2 = w2a - mu * w1
        w3 = v[3] - mu * v[2]
        w3 = w3 - mu * w2a
        w3 = w3 - mu * w2
        r = r3 * w3 + r2 * w2 + r1 * w1 + r0 * v[0]
        u = u2 * w2 + u1 * w1 + u0 * v[0]
        for z in range(CZ + 1):
            first = z * ZS + LOW
            inc[k, z] = u[LOW : LOW + CX, first : first + CY]
            res[k, z] = r[LOW : LOW + CX, first : first + CY]


VM = pl.BlockSpec(memory_space=pltpu.VMEM)
SM = pl.BlockSpec(memory_space=pltpu.SMEM)


def call(kernel, outs, ins, scratch=(), name=None):
    shapes = [jax.ShapeDtypeStruct(s, F32) for s in outs]
    specs = [SM if jnp.ndim(x) == 1 else VM for x in ins]
    return pl.pallas_call(
        kernel,
        out_shape=shapes,
        in_specs=specs,
        out_specs=[VM] * len(shapes),
        scratch_shapes=list(scratch),
        name=name,
        compiler_params=pltpu.CompilerParams(vmem_limit_bytes=48 * 2**20),
    )(*ins)


def upward(x, axis):
    n = lax.axis_size(axis)
    return lax.ppermute(x, axis, [(i, i + 1) for i in range(n - 1)])


def downward(x, axis):
    n = lax.axis_size(axis)
    return lax.ppermute(x, axis, [(i + 1, i) for i in range(n - 1)])


def body(reference_image, moving_image, image_gradient, voxel_shift, subvoxel):
    gz = moving_image.shape[0]
    shift = voxel_shift.reshape(-1)
    frac = subvoxel.reshape(-1)
    last = jnp.stack(
        [
            (lax.axis_index(GX) == lax.axis_size(GX) - 1).astype(jnp.int32),
            (lax.axis_index(GY) == lax.axis_size(GY) - 1).astype(jnp.int32),
        ]
    )

    mx_low = upward(moving_image[:, 24:32, :], GX)
    mx_up = downward(moving_image[:, 0:8, :], GX)

    own, s_up, s_low = call(
        stiff_kernel,
        [(6, ROWS, 384), (6, 32, 384), (6, 32, 384)],
        [image_gradient, bf(stiff_y_weights()), bf(stiff_x_weights())],
        [pltpu.VMEM((6 * 96, CZ * 128), F32)],
        name="stiff",
    )
    sx_low = upward(s_up, GX)
    sx_up = downward(s_low, GX)

    strip_up, strip_low = call(strip_kernel, [(3, 48, 128)] * 2, [moving_image, mx_low, mx_up], name="strip")
    my_low = upward(strip_up, GY)
    my_up = downward(strip_low, GY)

    plo, phi = place_x()
    ext, p_up, p_low = call(
        extend_kernel,
        [(6, ROWS, 384), (2, ROWS, 128), (2, ROWS, 128)],
        [own, sx_low, sx_up, bf(plo), bf(phi), bf(pack_y())],
        name="extend",
    )
    py_low = upward(p_up, GY)
    py_up = downward(p_low, GY)

    (load,) = call(
        warp_kernel,
        [(3, 8, 128)],
        [shift, frac, moving_image, mx_low, mx_up, my_low, my_up, reference_image, image_gradient,
         bf(load_y_weights()), bf(load_x_weights())],
        [pltpu.VMEM((2, gz, 48, 128), F32), pltpu.VMEM((96, 2 * CZ * 128), F32)],
        name="warp",
    )
    lx_low = upward(load, GX)
    lx_up = downward(load, GX)
    pad = lambda x, a, b: jnp.pad(x, ((0, 0), (a, b), (0, 0)))
    v_own = pad(load, 0, 8) + pad(lx_low[:, 4:8], 0, 12) + pad(lx_up[:, 3:6], 7, 6)
    v_low = upward(v_own, GY)
    v_up = downward(v_own, GY)

    nx, ny = lax.axis_size(GX), lax.axis_size(GY)
    basis, sums = call(
        krylov_kernel,
        [(4, 3, 8, 128), (nx, 128)],
        [last, v_own, v_low, v_up, ext, py_low, py_up, bf(place_y())],
        [pltpu.VMEM((6 * ROWS, 384), F32)],
        name="krylov",
    )
    rows = lax.all_to_all(sums, GX, 0, 0, tiled=True)
    (sums,) = call(partial_kernel, [(ny, 128)], [rows], name="partial")
    rows = lax.all_to_all(sums, GY, 0, 0, tiled=True)
    inc, res = call(finish_kernel, [(3, CZ + 1, CX, CY)] * 2, [rows, basis], name="finish")
    return inc, res


def solution(mesh, shape=(4, 2, 4, 8)):
    torus = Mesh(mesh.devices.reshape(shape), GX + GY)
    placed = (
        P(None, GX, GY),
        P(None, GX, GY),
        P(None, None, GX, GY),
        P(None, None, GX, GY),
        P(None, None, GX, GY),
    )
    return jax.shard_map(
        body,
        mesh=torus,
        in_specs=placed,
        out_specs=(P(None, None, GX, GY), P(None, None, GX, GY)),
        check_vma=False,
    )
```
